256 devices in a mesh: wide: 32 (over z_lo, y, core), narrow: 8 (over z_hi, x).
Axes of the slice: x: 4, y: 4, z: 8 (z_hi: 2, z_lo: 4; z = z_hi * 4 + z_lo), core: 2. Of those that a mesh axis runs over, the one named last changes fastest.
Arguments:
- gradient: float32 [3072, 3072], P('wide', 'narrow'), may hold values from -6 to 6
- first_moment: float32 [3072, 3072], P('wide', 'narrow'), may hold values from -6 to 6
- second_moment: float32 [3072, 3072], P('wide', 'narrow'), may hold values from 0.25 to 4
- left_basis: float32 [3072, 3072], P('wide', 'narrow'), may hold values from -0.21875 to 0.21875
- right_basis: float32 [3072, 3072], P('wide', 'narrow'), may hold values from -0.109375 to 0.109375
Outputs:
- update: float32 [3072, 3072], P('wide', 'narrow')
- new_first: float32 [3072, 3072], P('wide', 'narrow')
- new_second: float32 [3072, 3072], P('wide', 'narrow')
The draws below stay inside these ranges and needn't reach their ends.
All inputs are finite; a program needn't handle non-finite values.
Results may differ from the reference program's by a relative error of at most 0.000075.
Values sent between devices are 32-bit elements; how exact they have to be, the bound alone decides.
No kernel may reach another device: no remote copies, remote signals or barrier semaphores. Data moves between devices by JAX's collectives and lax.ppermute only.
A program may use at most 64 MiB of HBM per device.

```python
import math
import jax
import jax.numpy as jnp
from jax import lax

M = 3072
N = 3072
STEP = 10


def strengthened(drawn, stream_key, source, target, blocks, factor):
    def block_of(position):
        return (jnp.arange(drawn.shape[position]) // (drawn.shape[position] // blocks)).reshape((-1,) + (1,) * (drawn.ndim - 1 - position))

    first = jax.random.permutation(stream_key, blocks)[block_of(target)]
    far = (block_of(target) + blocks // 2) % blocks
    return jnp.where((block_of(source) == first) | (block_of(source) == far), factor * drawn, drawn)


def shard_levels(own_key, dims, cuts, low, high):
    gain = 1.0
    for dim, parts in cuts:
        steps = jax.random.uniform(jax.random.fold_in(jax.random.fold_in(own_key, 6), dim), (parts,), jnp.float32, low / len(cuts), high / len(cuts))
        gain = gain * jnp.repeat(jnp.exp(steps), dims[dim] // parts).reshape((-1,) + (1,) * (len(dims) - 1 - dim))
    return gain


def bell_draw(own_key, dims, scale, bound, cuts=(), held_as=jnp.bfloat16):
    values = scale * jax.random.normal(own_key, dims, jnp.float32)
    if cuts:
        values = values * shard_levels(own_key, dims, cuts, -0.22, 0.18)
    return jnp.clip(values, -bound, bound).astype(held_as)


def heavy_noise(key, dims, scale, most, shards, heavy, held_as=jnp.bfloat16):
    values = scale * jax.random.normal(key, dims, jnp.float32)
    if shards:
        values = values * shard_levels(key, dims, shards, -0.22, 0.18)
    return jnp.clip(strengthened(values, jax.random.fold_in(key, 3), *heavy), -most, most).astype(held_as)


def setup_inputs(seed: int = 0) -> dict:
    splits = jax.random.split(jax.random.key(seed), 6)
    return {
        "gradient": bell_draw(splits[0], (M, N), 1.0, 6.0, ((0, 32), (1, 8)), jnp.float32),
        "first_moment": bell_draw(splits[1], (M, N), 1.0, 6.0, ((0, 32), (1, 8)), jnp.float32),
        "second_moment": jnp.clip(jnp.exp(math.log(4.0) - 2.7725887 * jax.random.uniform(splits[2], (M, N), jnp.float32) ** shard_levels(splits[2], (M, N), ((0, 32), (1, 8)), -0.2, 0.2)), 0.25, 4.0),
        "left_basis": heavy_noise(splits[3], (M, M), M ** -0.5, 0.21875, ((0, 32), (1, 8)), (0, 1, 32, 2.75), jnp.float32),
        "right_basis": bell_draw(splits[4], (N, N), N ** -0.5, 0.109375, ((0, 32), (1, 8)), jnp.float32),
    }


beta_first = 0.9
beta_second = 0.95
epsilon = 1e-08

def product(left, right):
    return jnp.dot(left, right, precision=lax.Precision.HIGHEST, preferred_element_type=jnp.float32)

def reference(gradient, first_moment, second_moment, left_basis, right_basis):
    rotated_right = product(gradient, right_basis)
    rotated = product(left_basis.T, rotated_right)
    new_first = beta_first * first_moment + (1.0 - beta_first) * rotated
    new_second = beta_second * second_moment + (1.0 - beta_second) * rotated * rotated
    direction = new_first / (1.0 - beta_first ** STEP) / (jnp.sqrt(new_second / (1.0 - beta_second ** STEP)) + epsilon)
    back_left = product(left_basis, direction)
    update = product(back_left, right_basis.T)
    return (update, new_first, new_second)
```

```python
import jax
import jax.numpy as jnp
from jax import lax
from jax.sharding import Mesh
from jax.sharding import PartitionSpec as P

STEP = 10
WIDE = ("zl", "y", "c")
NARROW = ("zh", "x")

beta_first = 0.9
beta_second = 0.95
epsilon = 1e-08


def shift(value, axis, by):
    n = lax.axis_size(axis)
    return lax.ppermute(value, axis, [(i, (i + by) % n) for i in range(n)])


def ordered(flag, first, second):
    return jnp.where(
        flag == 0, jnp.stack([first, second]), jnp.stack([second, first])
    )


def dot(left, right, left_dim, right_dim):
    return lax.dot_general(
        left,
        right,
        (((left_dim,), (right_dim,)), ((), ())),
        precision=lax.Precision.HIGH,
        preferred_element_type=jnp.float32,
    )


def body(gradient, first_moment, second_moment, left_basis, right_basis):
    zl, y, c = (lax.axis_index(a) for a in WIDE)
    zh, x = (lax.axis_index(a) for a in NARROW)
    rows, cols = gradient.shape
    half, quarter = cols // 2, cols // 4

    def pick(value, which):
        return lax.dynamic_slice_in_dim(value, which * half, half, 1)

    def to_core_columns(value):
        other = shift(pick(value, 1 - c), "c", 1)
        return ordered(c, pick(value, c), other).reshape(2 * rows, half)

    def to_core_rows(value):
        tiles = value.reshape(2, rows, half)
        other = shift(lax.dynamic_index_in_dim(tiles, 1 - c, 0, False), "c", 1)
        own = lax.dynamic_index_in_dim(tiles, c, 0, False)
        return jnp.where(
            c == 0,
            jnp.concatenate([own, other], 1),
            jnp.concatenate([other, own], 1),
        )

    right_z = [right_basis] + [shift(right_basis, "zl", d) for d in (1, 2, 3)]
    right = jnp.zeros((16, rows, cols), jnp.float32)
    for dz in range(4):
        for dy in range(4):
            part = right_z[dz] if dy == 0 else shift(right_z[dz], "y", dy)
            at = ((zl - dz) % 4) * 4 + (y - dy) % 4
            right = lax.dynamic_update_slice(right, part[None], (at, 0, 0))

    tiles = gradient.reshape(rows, 2, 2, quarter)
    kept = jnp.where(c == 0, tiles[:, :, 0], tiles[:, :, 1]).reshape(rows, half)
    sent = jnp.where(c == 0, tiles[:, :, 1], tiles[:, :, 0]).reshape(rows, half)
    grad = ordered(c, kept, shift(sent, "c", 1)).reshape(2 * rows, half)
    grad = ordered(zh, grad, shift(grad, "zh", 1))
    grads = jnp.zeros((4, 2, 2 * rows, half), jnp.float32)
    for dx in range(4):
        part = grad if dx == 0 else shift(grad, "x", dx)
        grads = lax.dynamic_update_slice(grads, part[None], ((x - dx) % 4, 0, 0, 0))
    grads = grads.transpose(2, 1, 0, 3).reshape(2 * rows, 8 * half)

    tall = jnp.stack([left_basis[:, :half], left_basis[:, half:]])
    valid = (y // 2) == (x % 2)
    lefts = []
    for d in range(4):
        part = lax.dynamic_index_in_dim(tall, (y - d) % 2, 0, False)
        if d:
            pairs = [
                (a * 4 + b, ((a - d) % 4) * 4 + b)
                for a in range(4)
                for b in range(4)
                if ((a - d) % 4) // 2 == b % 2
            ]
            part = lax.ppermute(part, ("y", "x"), pairs)
        lefts.append(part)
    left = jnp.stack(lefts)
    left = ordered(zh, left, shift(left, "zh", 1))

    def from_sources(value, by):
        pairs = [
            (a * 4 + b, a * 4 + (b + by) % 4)
            for a in range(4)
            for b in range(4)
            if a // 2 == b % 2
        ]
        return lax.ppermute(value, ("y", "x"), pairs)

    up, down, over = (from_sources(left, by) for by in (1, -1, 2))
    near = jnp.where(valid, left, up)
    far = jnp.where(valid, over, down)
    which = jnp.where(valid, x, (x - 1) % 4) // 2
    left = ordered(which, near, far)
    left = ordered(c, left, shift(left, "c", 1))
    left = left.transpose(2, 1, 3, 0, 4, 5).reshape(4, 8 * rows, half)
    left = lax.dynamic_slice_in_dim(jnp.concatenate([left, left]), zl, 4, 0)

    first = to_core_columns(first_moment)
    second = to_core_columns(second_moment)

    partial = dot(grads, right.reshape(16 * rows, cols), 1, 0)
    rotated_right = pick(partial, c) + shift(pick(partial, 1 - c), "c", 1)
    panel = jnp.concatenate(
        [rotated_right] + [shift(rotated_right, "y", -d) for d in (1, 2, 3)]
    )
    terms = [shift(dot(left[e], panel, 0, 0), "zl", e) for e in (1, 2, 3)]
    rotated = dot(left[0], panel, 0, 0) + terms[0] + terms[1] + terms[2]

    new_first = beta_first * first + (1.0 - beta_first) * rotated
    new_second = beta_second * second + (1.0 - beta_second) * rotated * rotated
    direction = (
        new_first
        / (1.0 - beta_first**STEP)
        / (jnp.sqrt(new_second / (1.0 - beta_second**STEP)) + epsilon)
    )

    directions = [direction] + [shift(direction, "zl", -e) for e in (1, 2, 3)]
    back = sum(dot(left[e], directions[e], 1, 0) for e in range(4))
    back = back.reshape(4, 2 * rows, half)
    back = back[0] + sum(shift(back[d], "y", d) for d in (1, 2, 3))
    back = to_core_rows(back)

    both = ordered(c, right, shift(right, "c", 1)).transpose(1, 0, 2, 3)
    both = both.reshape(2, 4, cols, cols)

    def summed(which_zh):
        total = None
        for f in (1, 2, 3, 0):
            block = lax.dynamic_slice(
                both, (which_zh, (x + f) % 4, 0, 0), (1, 1, cols, cols)
            )[0, 0]
            term = dot(back, block, 1, 1)
            term = shift(term, "x", f) if f else term
            total = term if total is None else total + term
        return total

    away = shift(summed(1 - zh), "zh", 1)
    update = summed(zh) + away
    return (update, to_core_rows(new_first), to_core_rows(new_second))


def solution(mesh):
    torus = Mesh(mesh.devices.reshape(4, 4, 2, 2, 4), WIDE + NARROW)
    spec = P(WIDE, NARROW)
    return jax.shard_map(
        body,
        mesh=torus,
        in_specs=(spec,) * 5,
        out_specs=(spec,) * 3,
        check_vma=False,
    )
```

```python
import jax
import jax.numpy as jnp
from jax import lax
from jax.experimental import pallas as pl
from jax.experimental.pallas import tpu as pltpu
from jax.sharding import Mesh
from jax.sharding import PartitionSpec as P

STEP = 10
WIDE = ("zl", "y", "c")
NARROW = ("zh", "x")

beta_first = 0.9
beta_second = 0.95
epsilon = 1e-08

F32 = jnp.float32
BF16 = jnp.bfloat16


def shift(value, axis, by):
    n = lax.axis_size(axis)
    return lax.ppermute(value, axis, [(i, (i + by) % n) for i in range(n)])


def ordered(flag, first, second):
    return jnp.where(
        flag == 0, jnp.stack([first, second]), jnp.stack([second, first])
    )


def split(value):
    high = value.astype(BF16)
    return high, (value - high.astype(F32)).astype(BF16)


def product(left, right, dims=(1, 0)):
    def one(a, b):
        return lax.dot_general(
            a, b, (((dims[0],), (dims[1],)), ((), ())), preferred_element_type=F32
        )

    return one(left[0], right[0]) + (one(left[0], right[1]) + one(left[1], right[0]))


def call(kernel, place, arrays, outs, scratch=()):
    return pl.pallas_call(
        kernel,
        out_shape=outs,
        in_specs=[pl.BlockSpec(memory_space=pltpu.SMEM)]
        + [pl.BlockSpec(memory_space=pltpu.VMEM)] * len(arrays),
        out_specs=[pl.BlockSpec(memory_space=pltpu.VMEM)] * len(outs),
        scratch_shapes=scratch,
        compiler_params=pltpu.CompilerParams(vmem_limit_bytes=48 * 2**20),
    )(place, *arrays)


def shape(*lengths, dtype=F32):
    return jax.ShapeDtypeStruct(lengths, dtype)


ZL, Y, C, ZH, X = range(5)


def rotate_right_kernel(place, *refs):
    grads, rights = refs[:4], refs[4:8]
    mine, other, right, g_high, g_low = refs[8:]
    rows, cols = right.shape[1], right.shape[2]
    for dy in range(4):
        for dz in range(4):
            at = lax.rem(place[ZL] + 4 - dz, 4) * 4 + lax.rem(place[Y] + 4 - dy, 4)
            right[at] = rights[dy][dz]
    for dx in range(4):
        for r in range(2):
            zh = lax.rem(place[ZH] + r, 2)
            at = zh * 4 + lax.rem(place[X] + 4 - dx, 4)
            g_high[at], g_low[at] = split(grads[dx][r])
    total = None
    for k in range(8):
        block = right[2 * k : 2 * k + 2].reshape(2 * rows, cols)
        term = product((g_high[k], g_low[k]), split(block))
        total = term if total is None else total + term
    first = place[C] == 0
    half = cols // 2
    mine[...] = jnp.where(first, total[:, :half], total[:, half:])
    other[...] = jnp.where(first, total[:, half:], total[:, :half])


def pack_kernel(place, *refs):
    lefts, outs = refs[:4], refs[4:8]
    (stack,) = refs[8:]
    half = outs[0].shape[-1]
    for dx in range(4):
        stack[lax.rem(place[X] + 4 - dx, 4)] = lefts[dx][...]
    for d in range(4):
        y = lax.rem(place[Y] + 4 - d, 4)
        for t in range(2):
            tile = stack[2 * t + lax.div(y, 2)]
            outs[d][t] = jnp.where(
                lax.rem(y, 2) == 0, tile[:, :, :half], tile[:, :, half:]
            )


def left_kernel(place, own, away, high, low, t_high, t_low):
    rows, half = own.shape[-2:]
    for e in range(4):
        a = lax.rem(place[ZL] + e, 4)
        r = lax.rem(lax.div(a, 2) + place[ZH], 2)
        t = lax.rem(a, 2)
        for d in range(4):
            mine, theirs = own[d, t, r], away[d, t, r]
            first = place[C] == 0
            tile = jnp.concatenate(
                [jnp.where(first, mine, theirs), jnp.where(first, theirs, mine)]
            )
            h, l = split(tile)
            high[e, 2 * rows * d : 2 * rows * (d + 1)] = h
            low[e, 2 * rows * d : 2 * rows * (d + 1)] = l
            turned = tile.T
            h, l = split(turned)
            t_high[d, half * e : half * (e + 1)] = h
            t_low[d, half * e : half * (e + 1)] = l


def rotate_left_kernel(place, *refs):
    t_high, t_low = refs[:2]
    panels, outs = refs[2:6], refs[6:]
    half = outs[0].shape[0]
    parts = [split(p[...]) for p in panels]
    for e in range(4):
        total = None
        for d in range(4):
            at = slice(half * e, half * (e + 1))
            term = product((t_high[d, at], t_low[d, at]), parts[d])
            total = term if total is None else total + term
        outs[e][...] = total


def back_left_kernel(place, *refs):
    high, low = refs[:2]
    panels, outs = refs[2:6], refs[6:]
    size = outs[0].shape[0]
    parts = [split(p[...]) for p in panels]
    for d in range(4):
        total = None
        for e in range(4):
            at = slice(size * d, size * (d + 1))
            term = product((high[e, at], low[e, at]), parts[e])
            total = term if total is None else total + term
        outs[d][...] = total


def right_kernel(place, own, away, high, low):
    rows = own.shape[1]
    for s in range(16):
        first = place[C] == 0
        mine, theirs = own[s], away[s]
        tile = jnp.concatenate(
            [jnp.where(first, mine, theirs), jnp.where(first, theirs, mine)]
        )
        at = slice(2 * rows * (s % 2), 2 * rows * (s % 2 + 1))
        high[s // 2, at], low[s // 2, at] = split(tile)


def back_right_kernel(place, back, high, low, *outs):
    left = split(back[...])
    for r in range(2):
        zh = lax.rem(place[ZH] + 1 + r, 2)
        for f in range(4):
            k = zh * 4 + lax.rem(place[X] + f, 4)
            outs[4 * r + f][...] = product(left, (high[k], low[k]), (1, 1))


def body(gradient, first_moment, second_moment, left_basis, right_basis):
    zl, y, c = (lax.axis_index(a) for a in WIDE)
    zh, x = (lax.axis_index(a) for a in NARROW)
    place = jnp.stack([zl, y, c, zh, x]).astype(jnp.int32)
    rows, cols = gradient.shape
    half, quarter = cols // 2, cols // 4
    size = 2 * rows

    def halves(value):
        first = c == 0
        return (
            jnp.where(first, value[:, :half], value[:, half:]),
            jnp.where(first, value[:, half:], value[:, :half]),
        )

    def to_core_rows(value):
        first = c == 0
        top, bottom = value[:rows], value[rows:]
        other = shift(jnp.where(first, bottom, top), "c", 1)
        own = jnp.where(first, top, bottom)
        return jnp.where(
            first,
            jnp.concatenate([own, other], 1),
            jnp.concatenate([other, own], 1),
        )

    tiles = gradient.reshape(rows, 2, 2, quarter)
    even = tiles[:, :, 0].reshape(rows, half)
    odd = tiles[:, :, 1].reshape(rows, half)
    kept = [(jnp.where(c == 0, even, odd), jnp.where(c == 0, odd, even))]
    kept += [halves(first_moment), halves(second_moment)]
    swapped = shift(jnp.stack([k[1] for k in kept]), "c", 1)
    grad, first, second = (
        ordered(c, kept[i][0], swapped[i]).reshape(size, half) for i in range(3)
    )

    right_z = jnp.stack(
        [right_basis] + [shift(right_basis, "zl", d) for d in (1, 2, 3)]
    )
    right_parts = [right_z] + [shift(right_z, "y", d) for d in (1, 2, 3)]

    grad = jnp.stack([grad, shift(grad, "zh", 1)])
    grad_parts = [grad] + [shift(grad, "x", d) for d in (1, 2, 3)]

    left, _ = lax.optimization_barrier((left_basis, grad))
    left = jnp.stack([left, shift(left, "zh", 1)])
    left_parts = [left] + [shift(left, "x", d) for d in (1, 2, 3)]
    packed = call(
        pack_kernel,
        place,
        left_parts,
        [shape(2, 2, rows, half)] * 4,
        [pltpu.VMEM((4, 2, rows, cols), F32)],
    )
    left = jnp.stack([packed[0]] + [shift(packed[d], "y", -d) for d in (1, 2, 3)])
    block = size * 4
    lefts = call(
        left_kernel,
        place,
        [left, shift(left, "c", 1)],
        [shape(4, block, half, dtype=BF16)] * 2
        + [shape(4, 4 * half, size, dtype=BF16)] * 2,
    )

    mine, other, right = call(
        rotate_right_kernel,
        place,
        grad_parts + right_parts,
        [shape(size, half)] * 2 + [shape(16, rows, cols)],
        [pltpu.VMEM((8, size, half), BF16)] * 2,
    )
    rotated_right = mine + shift(other, "c", 1)
    panels = [rotated_right] + [shift(rotated_right, "y", -d) for d in (1, 2, 3)]
    terms = call(
        rotate_left_kernel, place, list(lefts[2:]) + panels, [shape(half, half)] * 4
    )
    rotated = terms[0] + sum(shift(terms[e], "zl", e) for e in (1, 2, 3))

    rights = call(
        right_kernel,
        place,
        [right, shift(right, "c", 1)],
        [shape(8, cols, cols, dtype=BF16)] * 2,
    )

    new_first = beta_first * first + (1.0 - beta_first) * rotated
    new_second = beta_second * second + (1.0 - beta_second) * rotated * rotated
    direction = (
        new_first
        / (1.0 - beta_first**STEP)
        / (jnp.sqrt(new_second / (1.0 - beta_second**STEP)) + epsilon)
    )

    directions = [direction] + [shift(direction, "zl", -e) for e in (1, 2, 3)]
    back = call(
        back_left_kernel,
        place,
        list(lefts[:2]) + directions,
        [shape(size, half)] * 4,
    )
    back = back[0] + sum(shift(back[d], "y", d) for d in (1, 2, 3))
    back = to_core_rows(back)

    parts = call(
        back_right_kernel, place, [back, *rights], [shape(rows, cols)] * 8
    )

    def summed(values):
        return values[0] + sum(shift(values[f], "x", f) for f in (1, 2, 3))

    update = summed(parts[4:]) + shift(summed(parts[:4]), "zh", 1)
    return (update, to_core_rows(new_first), to_core_rows(new_second))


def solution(mesh):
    torus = Mesh(mesh.devices.reshape(4, 4, 2, 2, 4), WIDE + NARROW)
    spec = P(WIDE, NARROW)
    return jax.shard_map(
        body,
        mesh=torus,
        in_specs=(spec,) * 5,
        out_specs=(spec,) * 3,
        check_vma=False,
    )
```

```python
import functools

import jax
import jax.numpy as jnp
from jax import lax
from jax.experimental import pallas as pl
from jax.experimental.pallas import tpu as pltpu
from jax.sharding import Mesh
from jax.sharding import PartitionSpec as P

STEP = 10
WIDE = ("zl", "y", "c")
NARROW = ("zh", "x")

beta_first = 0.9
beta_second = 0.95
epsilon = 1e-08

F32 = jnp.float32
BF16 = jnp.bfloat16


def shift(value, axis, by):
    n = lax.axis_size(axis)
    return lax.ppermute(value, axis, [(i, (i + by) % n) for i in range(n)])


def split(value):
    high = value.astype(BF16)
    return high, (value - high.astype(F32)).astype(BF16)


def product(left, right, dims=(1, 0)):
    def one(a, b):
        return lax.dot_general(
            a, b, (((dims[0],), (dims[1],)), ((), ())), preferred_element_type=F32
        )

    return one(left[0], right[0]) + (one(left[0], right[1]) + one(left[1], right[0]))


def call(kernel, place, arrays, outs, scratch=()):
    return pl.pallas_call(
        kernel,
        out_shape=outs,
        in_specs=[pl.BlockSpec(memory_space=pltpu.SMEM)]
        + [pl.BlockSpec(memory_space=pltpu.VMEM)] * len(arrays),
        out_specs=[pl.BlockSpec(memory_space=pltpu.VMEM)] * len(outs),
        scratch_shapes=scratch,
        compiler_params=pltpu.CompilerParams(vmem_limit_bytes=20 * 2**20),
    )(place, *arrays)


def shape(*lengths, dtype=F32):
    return jax.ShapeDtypeStruct(lengths, dtype)


ZL, Y, C, ZH, X = range(5)


def packed(value):
    rows, half = value.shape[0] // 2, value.shape[1]
    return (slice(0, half), value[:rows]), (slice(half, 2 * half), value[rows:])


def store(ref, value):
    for lanes, part in packed(value):
        ref[:, lanes] = part


def load(ref):
    half = ref.shape[1] // 2
    return split(jnp.concatenate([ref[:, :half], ref[:, half:]]))


def core_columns(tile, which):
    q = tile.shape[1] // 4
    even = jnp.concatenate([tile[:, :q], tile[:, 2 * q : 3 * q]], 1)
    odd = jnp.concatenate([tile[:, q : 2 * q], tile[:, 3 * q :]], 1)
    return jnp.where(which == 0, even, odd)


def pack_gradient_kernel(place, own, away, out):
    half = out.shape[1] // 2
    first = place[C] == 0
    mine = core_columns(own[...], place[C])
    theirs = core_columns(away[...], place[C])
    out[:, :half] = jnp.where(first, mine, theirs)
    out[:, half:] = jnp.where(first, theirs, mine)


def rotate_right_kernel(place, *refs):
    grads, nears, fars = refs[:4], refs[4:8], refs[8:12]
    mine, other, right, g_high, g_low = refs[12:]
    rows, cols = right.shape[1], right.shape[2]
    half = cols // 2
    first = place[C] == 0
    for dy in range(4):
        for dz in range(4):
            at = lax.rem(place[ZL] + 4 - dz, 4) * 4 + lax.rem(place[Y] + 4 - dy, 4)
            right[at] = fars[dy][dz - 1] if dz else nears[dy][...]
    for dx in range(4):
        x = lax.rem(place[X] + 4 - dx, 4)
        for r in range(2):
            at = lax.rem(place[ZH] + r, 2) * 4 + x
            tile = jnp.concatenate([grads[dx][r, :, :half], grads[dx][r, :, half:]])
            g_high[at], g_low[at] = split(tile)
    total = None
    for k in range(8):
        block = right[2 * k : 2 * k + 2].reshape(2 * rows, cols)
        term = product((g_high[k], g_low[k]), split(block))
        total = term if total is None else total + term
    store(mine, jnp.where(first, total[:, :half], total[:, half:]))
    store(other, jnp.where(first, total[:, half:], total[:, :half]))


def pack_left_kernel(place, *refs):
    lefts, outs = refs[:4], refs[4:8]
    (stack,) = refs[8:]
    half = outs[0].shape[-1] // 2
    for dx in range(4):
        stack[lax.rem(place[X] + 4 - dx, 4)] = lefts[dx][...]
    for d in range(4):
        y = lax.rem(place[Y] + 4 - d, 4)
        for t in range(2):
            tile = stack[2 * t + lax.div(y, 2)]
            outs[d][:, half * t : half * (t + 1)] = jnp.where(
                lax.rem(y, 2) == 0, tile[:, :half], tile[:, half:]
            )


def left_kernel(place, *refs):
    owns, aways = refs[:2], refs[2:4]
    high, low, t_high, t_low = refs[4:]
    rows, half = owns[0].shape[1], owns[0].shape[2] // 2
    first = place[C] == 0
    for r in range(2):
        for t in range(2):
            a = 2 * lax.rem(place[ZH] + r, 2) + t
            e = lax.rem(a + 4 - place[ZL], 4)
            for d in range(4):
                lanes = slice(half * t, half * (t + 1))
                mine, theirs = owns[r][d, :, lanes], aways[r][d, :, lanes]
                tile = jnp.concatenate(
                    [jnp.where(first, mine, theirs), jnp.where(first, theirs, mine)]
                )
                high[e, d], low[e, d] = split(tile)
                t_high[e, d], t_low[e, d] = split(tile.T)


def rotate_left_kernel(place, *refs):
    t_high, t_low = refs[:2]
    panels, outs = refs[2:6], refs[6:]
    parts = [load(p) for p in panels]
    for e in range(4):
        total = None
        for d in range(4):
            term = product((t_high[e, d], t_low[e, d]), parts[d])
            total = term if total is None else total + term
        store(outs[e], total)


def back_left_kernel(place, *refs):
    high, low = refs[:2]
    panels, outs = refs[2:6], refs[6:]
    parts = [load(p) for p in panels]
    for d in range(4):
        total = None
        for e in range(4):
            term = product((high[e, d], low[e, d]), parts[e])
            total = term if total is None else total + term
        store(outs[d], total)


def right_kernel(place, own, away, high, low):
    rows = own.shape[1]
    for s in range(16):
        first = place[C] == 0
        mine, theirs = own[s], away[s]
        tile = jnp.concatenate(
            [jnp.where(first, mine, theirs), jnp.where(first, theirs, mine)]
        )
        at = slice(2 * rows * (s % 2), 2 * rows * (s % 2 + 1))
        high[s // 2, at], low[s // 2, at] = split(tile)


def back_right_kernel(r, place, back, high, low, *outs):
    left = split(back[...])
    zh = lax.rem(place[ZH] + r, 2)
    for f in range(4):
        k = zh * 4 + lax.rem(place[X] + f, 4)
        outs[f][...] = product(left, (high[k], low[k]), (1, 1))


def gathered(value, axis, by=1):
    return [value] + [shift(value, axis, by * d) for d in (1, 2, 3)]


def body(gradient, first_moment, second_moment, left_basis, right_basis):
    zl, y, c = (lax.axis_index(a) for a in WIDE)
    zh, x = (lax.axis_index(a) for a in NARROW)
    place = jnp.stack([zl, y, c, zh, x]).astype(jnp.int32)
    rows, cols = gradient.shape
    half = cols // 2
    size = 2 * rows

    def swapped(value):
        one, two = value[..., :half], value[..., half:]
        first = c == 0
        other = shift(jnp.where(first, two, one), "c", 1)
        return jnp.concatenate(
            [jnp.where(first, one, other), jnp.where(first, other, two)], -1
        )

    nears = gathered(right_basis, "y")
    right_z = jnp.stack([shift(right_basis, "zl", d) for d in (1, 2, 3)])
    (grad,) = call(
        pack_gradient_kernel,
        place,
        [gradient, shift(gradient, "c", 1)],
        [shape(rows, cols)],
    )
    grad = jnp.stack([grad, shift(grad, "zh", 1)])
    left_parts = gathered(left_basis, "x")

    packs = call(pack_left_kernel, place, left_parts, [shape(rows, cols)] * 4,
                 [pltpu.VMEM((4, rows, cols), F32)])
    left = jnp.stack([packs[0]] + [shift(packs[d], "y", -d) for d in (1, 2, 3)])

    grad, right_z = lax.optimization_barrier((grad, right_z))
    fars = gathered(right_z, "y")
    grad_parts = gathered(grad, "x")

    left, _ = lax.optimization_barrier((left, right_z))
    lefts = [left, shift(left, "zh", 1)]
    fars[1], lefts[1] = lax.optimization_barrier((fars[1], lefts[1]))
    lefts = call(
        left_kernel,
        place,
        lefts + [shift(part, "c", 1) for part in lefts],
        [shape(4, 4, size, half, dtype=BF16)] * 2
        + [shape(4, 4, half, size, dtype=BF16)] * 2,
    )

    mine, other, right = call(
        rotate_right_kernel,
        place,
        grad_parts + nears + fars,
        [shape(rows, cols)] * 2 + [shape(16, rows, cols)],
        [pltpu.VMEM((8, size, half), BF16)] * 2,
    )
    rotated_right = mine + shift(other, "c", 1)
    panels = gathered(rotated_right, "y", -1)
    terms = call(
        rotate_left_kernel, place, list(lefts[2:]) + panels, [shape(rows, cols)] * 4
    )
    rotated = terms[0] + sum(shift(terms[e], "zl", e) for e in (1, 2, 3))

    rights = call(
        right_kernel,
        place,
        [right, shift(right, "c", 1)],
        [shape(8, cols, cols, dtype=BF16)] * 2,
    )

    first, second = swapped(jnp.stack([first_moment, second_moment]))
    new_first = beta_first * first + (1.0 - beta_first) * rotated
    new_second = beta_second * second + (1.0 - beta_second) * rotated * rotated
    direction = (
        new_first
        / (1.0 - beta_first**STEP)
        / (jnp.sqrt(new_second / (1.0 - beta_second**STEP)) + epsilon)
    )
    moments = swapped(jnp.stack([new_first, new_second]))

    directions = gathered(direction, "zl", -1)
    lefts, rights = lax.optimization_barrier((lefts, rights))
    back = call(
        back_left_kernel, place, list(lefts[:2]) + directions, [shape(rows, cols)] * 4
    )
    back = swapped(back[0] + sum(shift(back[d], "y", d) for d in (1, 2, 3)))

    def summed(r):
        values = call(
            functools.partial(back_right_kernel, r),
            place,
            [back, *rights],
            [shape(rows, cols)] * 4,
        )
        return values[0] + sum(shift(values[f], "x", f) for f in (1, 2, 3))

    away = shift(summed(1), "zh", 1)
    update = summed(0) + away
    return (update, *moments)


def solution(mesh):
    torus = Mesh(mesh.devices.reshape(4, 4, 2, 2, 4), WIDE + NARROW)
    spec = P(WIDE, NARROW)
    return jax.shard_map(
        body,
        mesh=torus,
        in_specs=(spec,) * 5,
        out_specs=(spec,) * 3,
        check_vma=False,
    )
```

```python
import functools

import jax
import jax.numpy as jnp
from jax import lax
from jax.experimental import pallas as pl
from jax.experimental.pallas import tpu as pltpu
from jax.sharding import Mesh
from jax.sharding import PartitionSpec as P

STEP = 10
WIDE = ("zl", "y", "c")
NARROW = ("zh", "x")

beta_first = 0.9
beta_second = 0.95
epsilon = 1e-08

F32 = jnp.float32
BF16 = jnp.bfloat16


def shift(value, axis, by):
    n = lax.axis_size(axis)
    return lax.ppermute(value, axis, [(i, (i + by) % n) for i in range(n)])


def split(value):
    high = value.astype(BF16)
    return high, (value - high.astype(F32)).astype(BF16)


def product(left, right, dims=(1, 0)):
    def one(a, b):
        return lax.dot_general(
            a, b, (((dims[0],), (dims[1],)), ((), ())), preferred_element_type=F32
        )

    return one(left[0], right[0]) + (one(left[0], right[1]) + one(left[1], right[0]))


def call(kernel, place, arrays, outs, scratch=()):
    return pl.pallas_call(
        kernel,
        out_shape=outs,
        in_specs=[pl.BlockSpec(memory_space=pltpu.SMEM)]
        + [pl.BlockSpec(memory_space=pltpu.VMEM)] * len(arrays),
        out_specs=[pl.BlockSpec(memory_space=pltpu.VMEM)] * len(outs),
        scratch_shapes=scratch,
        compiler_params=pltpu.CompilerParams(vmem_limit_bytes=20 * 2**20),
    )(place, *arrays)


def shape(*lengths, dtype=F32):
    return jax.ShapeDtypeStruct(lengths, dtype)


ZL, Y, C, ZH, X = range(5)


def packed(value):
    rows, half = value.shape[0] // 2, value.shape[1]
    return (slice(0, half), value[:rows]), (slice(half, 2 * half), value[rows:])


def store(ref, value):
    for lanes, part in packed(value):
        ref[:, lanes] = part


def load(ref):
    half = ref.shape[1] // 2
    return split(jnp.concatenate([ref[:, :half], ref[:, half:]]))


def core_columns(tile, which):
    q = tile.shape[1] // 4
    even = jnp.concatenate([tile[:, :q], tile[:, 2 * q : 3 * q]], 1)
    odd = jnp.concatenate([tile[:, q : 2 * q], tile[:, 3 * q :]], 1)
    return jnp.where(which == 0, even, odd)


def pack_gradient_kernel(place, own, away, out):
    half = out.shape[1] // 2
    first = place[C] == 0
    mine = core_columns(own[...], place[C])
    theirs = core_columns(away[...], place[C])
    out[:, :half] = jnp.where(first, mine, theirs)
    out[:, half:] = jnp.where(first, theirs, mine)


def rotate_right_kernel(place, *refs):
    grads, rights = refs[:5], refs[5:10]
    mine, other, right, g_high, g_low = refs[10:]
    rows, cols = right.shape[1], right.shape[2]
    half = cols // 2
    first = place[C] == 0
    for dy in range(4):
        for dz in range(4):
            at = lax.rem(place[ZL] + 4 - dz, 4) * 4 + lax.rem(place[Y] + dy, 4)
            if dy == 2:
                right[at] = rights[3 + dz // 2][dz % 2]
            else:
                right[at] = rights[(0, 2, None, 1)[dy]][dz]
    for dx in range(4):
        x = lax.rem(place[X] + dx, 4)
        for r in range(2):
            at = lax.rem(place[ZH] + r, 2) * 4 + x
            if dx == 2:
                block = grads[3 + r][0]
            else:
                block = grads[(0, 2, None, 1)[dx]][r]
            tile = jnp.concatenate([block[:, :half], block[:, half:]])
            g_high[at], g_low[at] = split(tile)
    total = None
    for k in range(8):
        block = right[2 * k : 2 * k + 2].reshape(2 * rows, cols)
        term = product((g_high[k], g_low[k]), split(block))
        total = term if total is None else total + term
    store(mine, jnp.where(first, total[:, :half], total[:, half:]))
    store(other, jnp.where(first, total[:, half:], total[:, :half]))


def pack_left_kernel(place, stack, out):
    half = out.shape[-1] // 2
    for d in range(4):
        for t in range(2):
            tile = stack[2 * t + d // 2]
            lanes = slice(half * t, half * (t + 1))
            out[d, :, lanes] = tile[:, :half] if d % 2 == 0 else tile[:, half:]


def left_kernel(place, *refs):
    owns, aways = refs[:2], refs[2:4]
    high, low, t_high, t_low = refs[4:]
    rows, half = owns[0].shape[1], owns[0].shape[2] // 2
    first = place[C] == 0
    for r in range(2):
        for t in range(2):
            a = 2 * lax.rem(place[ZH] + r, 2) + t
            e = lax.rem(a + 4 - place[ZL], 4)
            for d in range(4):
                at = lax.rem(place[Y] + d, 4)
                lanes = slice(half * t, half * (t + 1))
                mine, theirs = owns[r][at, :, lanes], aways[r][at, :, lanes]
                tile = jnp.concatenate(
                    [jnp.where(first, mine, theirs), jnp.where(first, theirs, mine)]
                )
                high[e, d], low[e, d] = split(tile)
                t_high[e, d], t_low[e, d] = split(tile.T)


def rotate_left_kernel(place, *refs):
    t_high, t_low = refs[:2]
    panels, outs = refs[2:6], refs[6:]
    parts = [load(p) for p in panels]
    for e in range(4):
        total = None
        for d in range(4):
            term = product((t_high[e, d], t_low[e, d]), parts[d])
            total = term if total is None else total + term
        store(outs[e], total)


def back_left_kernel(place, *refs):
    high, low = refs[:2]
    panels, outs = refs[2:6], refs[6:]
    parts = [load(p) for p in panels]
    for d in range(4):
        total = None
        for e in range(4):
            term = product((high[e, d], low[e, d]), parts[e])
            total = term if total is None else total + term
        store(outs[d], total)


def right_kernel(place, own, away, high, low):
    rows = own.shape[1]
    for s in range(16):
        first = place[C] == 0
        mine, theirs = own[s], away[s]
        tile = jnp.concatenate(
            [jnp.where(first, mine, theirs), jnp.where(first, theirs, mine)]
        )
        at = slice(2 * rows * (s % 2), 2 * rows * (s % 2 + 1))
        high[s // 2, at], low[s // 2, at] = split(tile)


def back_right_kernel(r, place, back, high, low, *outs):
    left = split(back[...])
    zh = lax.rem(place[ZH] + r, 2)
    for f in range(4):
        k = zh * 4 + lax.rem(place[X] + f, 4)
        outs[f][...] = product(left, (high[k], low[k]), (1, 1))


def copies_sent(value, axis):
    n = lax.axis_size(axis)
    copies = jnp.broadcast_to(value[None], (n, *value.shape))
    return lax.all_to_all(copies, axis, 0, 0, tiled=True)


def ring(value, axis, tie=None):
    n = value.shape[0] // 2
    up, down = shift(value, axis, 1), shift(value, axis, -1)
    if tie is not None:
        up, down, tie = lax.optimization_barrier((up, down, tie))
    far = [shift(up[:n], axis, 1), shift(down[n:], axis, -1)]
    return [value, up, down] + far


def gathered(value, axis, by=1):
    return [value] + [shift(value, axis, by * d) for d in (1, 2, 3)]


def body(gradient, first_moment, second_moment, left_basis, right_basis):
    zl, y, c = (lax.axis_index(a) for a in WIDE)
    zh, x = (lax.axis_index(a) for a in NARROW)
    place = jnp.stack([zl, y, c, zh, x]).astype(jnp.int32)
    rows, cols = gradient.shape
    half = cols // 2
    size = 2 * rows

    def swapped(value):
        one, two = value[..., :half], value[..., half:]
        first = c == 0
        other = shift(jnp.where(first, two, one), "c", 1)
        return jnp.concatenate(
            [jnp.where(first, one, other), jnp.where(first, other, two)], -1
        )

    right_z = jnp.stack(
        [right_basis] + [shift(right_basis, "zl", d) for d in (1, 2, 3)]
    )
    (grad,) = call(
        pack_gradient_kernel,
        place,
        [gradient, shift(gradient, "c", 1)],
        [shape(rows, cols)],
    )
    grad = jnp.stack([grad, shift(grad, "zh", 1)])
    grad, right_z = lax.optimization_barrier((grad, right_z))
    left_parts = copies_sent(left_basis, "x")

    (packs,) = call(pack_left_kernel, place, [left_parts], [shape(4, rows, cols)])
    left = lax.all_to_all(packs, "y", 0, 0, tiled=True)
    left, _ = lax.optimization_barrier((left, grad))

    right_parts = ring(right_z, "y")
    grad_parts = ring(grad, "x")
    left_far = shift(left, "zh", 1)
    both = shift(jnp.stack([left, left_far]), "c", 1)
    lefts = call(
        left_kernel,
        place,
        [left, left_far, both[0], both[1]],
        [shape(4, 4, size, half, dtype=BF16)] * 2
        + [shape(4, 4, half, size, dtype=BF16)] * 2,
    )

    mine, other, right = call(
        rotate_right_kernel,
        place,
        grad_parts + right_parts,
        [shape(rows, cols)] * 2 + [shape(16, rows, cols)],
        [pltpu.VMEM((8, size, half), BF16)] * 2,
    )
    other, _ = lax.optimization_barrier((other, left_far))
    rotated_right = mine + shift(other, "c", 1)
    panels = gathered(rotated_right, "y", -1)
    terms = call(
        rotate_left_kernel, place, list(lefts[2:]) + panels, [shape(rows, cols)] * 4
    )
    rotated = terms[0] + sum(shift(terms[e], "zl", e) for e in (1, 2, 3))

    rights = call(
        right_kernel,
        place,
        [right, shift(right, "c", 1)],
        [shape(8, cols, cols, dtype=BF16)] * 2,
    )

    first, second = swapped(jnp.stack([first_moment, second_moment]))
    new_first = beta_first * first + (1.0 - beta_first) * rotated
    new_second = beta_second * second + (1.0 - beta_second) * rotated * rotated
    direction = (
        new_first
        / (1.0 - beta_first**STEP)
        / (jnp.sqrt(new_second / (1.0 - beta_second**STEP)) + epsilon)
    )
    moments = swapped(jnp.stack([new_first, new_second]))

    directions = gathered(direction, "zl", -1)
    lefts, rights = lax.optimization_barrier((lefts, rights))
    back = call(
        back_left_kernel, place, list(lefts[:2]) + directions, [shape(rows, cols)] * 4
    )
    back = swapped(back[0] + sum(shift(back[d], "y", d) for d in (1, 2, 3)))

    def summed(r):
        values = call(
            functools.partial(back_right_kernel, r),
            place,
            [back, *rights],
            [shape(rows, cols)] * 4,
        )
        return values[0] + sum(shift(values[f], "x", f) for f in (1, 2, 3))

    away = shift(summed(1), "zh", 1)
    update = summed(0) + away
    return (update, *moments)


def solution(mesh):
    torus = Mesh(mesh.devices.reshape(4, 4, 2, 2, 4), WIDE + NARROW)
    spec = P(WIDE, NARROW)
    return jax.shard_map(
        body,
        mesh=torus,
        in_specs=(spec,) * 5,
        out_specs=(spec,) * 3,
        check_vma=False,
    )
```

```python
import functools

import jax
import jax.numpy as jnp
from jax import lax
from jax.experimental import pallas as pl
from jax.experimental.pallas import tpu as pltpu
from jax.sharding import Mesh
from jax.sharding import PartitionSpec as P

STEP = 10
WIDE = ("zl", "y", "c")
NARROW = ("zh", "x")

beta_first = 0.9
beta_second = 0.95
epsilon = 1e-08

F32 = jnp.float32
BF16 = jnp.bfloat16


def shift(value, axis, by):
    n = lax.axis_size(axis)
    return lax.ppermute(value, axis, [(i, (i + by) % n) for i in range(n)])


def split(value):
    high = value.astype(BF16)
    return high, (value - high.astype(F32)).astype(BF16)


def product(left, right, dims=(1, 0)):
    def one(a, b):
        return lax.dot_general(
            a, b, (((dims[0],), (dims[1],)), ((), ())), preferred_element_type=F32
        )

    return one(left[0], right[0]) + (one(left[0], right[1]) + one(left[1], right[0]))


def call(kernel, place, arrays, outs, scratch=()):
    return pl.pallas_call(
        kernel,
        out_shape=outs,
        in_specs=[pl.BlockSpec(memory_space=pltpu.SMEM)]
        + [pl.BlockSpec(memory_space=pltpu.VMEM)] * len(arrays),
        out_specs=[pl.BlockSpec(memory_space=pltpu.VMEM)] * len(outs),
        scratch_shapes=scratch,
        compiler_params=pltpu.CompilerParams(vmem_limit_bytes=20 * 2**20),
    )(place, *arrays)


def shape(*lengths, dtype=F32):
    return jax.ShapeDtypeStruct(lengths, dtype)


ZL, Y, C, ZH, X = range(5)


def packed(value):
    rows, half = value.shape[0] // 2, value.shape[1]
    return (slice(0, half), value[:rows]), (slice(half, 2 * half), value[rows:])


def store(ref, value):
    for lanes, part in packed(value):
        ref[:, lanes] = part


def load(ref):
    half = ref.shape[1] // 2
    return split(jnp.concatenate([ref[:, :half], ref[:, half:]]))


def core_columns(tile, which):
    q = tile.shape[1] // 4
    even = jnp.concatenate([tile[:, :q], tile[:, 2 * q : 3 * q]], 1)
    odd = jnp.concatenate([tile[:, q : 2 * q], tile[:, 3 * q :]], 1)
    return jnp.where(which == 0, even, odd)


def pack_gradient_kernel(place, own, away, out):
    half = out.shape[1] // 2
    first = place[C] == 0
    mine = core_columns(own[...], place[C])
    theirs = core_columns(away[...], place[C])
    out[:, :half] = jnp.where(first, mine, theirs)
    out[:, half:] = jnp.where(first, theirs, mine)


def rotate_right_kernel(place, *refs):
    grads, rights = refs[:5], refs[5:10]
    mine, other, right, g_high, g_low = refs[10:]
    rows, cols = right.shape[1], right.shape[2]
    half = cols // 2
    first = place[C] == 0
    for dy in range(4):
        for dz in range(4):
            at = lax.rem(place[ZL] + 4 - dz, 4) * 4 + lax.rem(place[Y] + dy, 4)
            if dy == 2:
                right[at] = rights[3 + dz // 2][dz % 2]
            else:
                right[at] = rights[(0, 2, None, 1)[dy]][dz]
    for dx in range(4):
        x = lax.rem(place[X] + dx, 4)
        for r in range(2):
            at = lax.rem(place[ZH] + r, 2) * 4 + x
            if dx == 2:
                block = grads[3 + r][0]
            else:
                block = grads[(0, 2, None, 1)[dx]][r]
            tile = jnp.concatenate([block[:, :half], block[:, half:]])
            g_high[at], g_low[at] = split(tile)
    total = None
    for k in range(8):
        block = right[2 * k : 2 * k + 2].reshape(2 * rows, cols)
        term = product((g_high[k], g_low[k]), split(block))
        total = term if total is None else total + term
    store(mine, jnp.where(first, total[:, :half], total[:, half:]))
    store(other, jnp.where(first, total[:, half:], total[:, :half]))


def pack_left_kernel(place, stack, out):
    half = out.shape[-1] // 2
    for d in range(4):
        for t in range(2):
            tile = stack[2 * t + d // 2]
            lanes = slice(half * t, half * (t + 1))
            out[d, :, lanes] = tile[:, :half] if d % 2 == 0 else tile[:, half:]


def left_kernel(place, *refs):
    owns, aways = refs[:2], refs[2:4]
    high, low, t_high, t_low = refs[4:]
    rows, half = owns[0].shape[1], owns[0].shape[2] // 2
    first = place[C] == 0
    for r in range(2):
        for t in range(2):
            a = 2 * lax.rem(place[ZH] + r, 2) + t
            e = lax.rem(a + 4 - place[ZL], 4)
            for d in range(4):
                at = lax.rem(place[Y] + d, 4)
                lanes = slice(half * t, half * (t + 1))
                mine, theirs = owns[r][at, :, lanes], aways[r][at, :, lanes]
                tile = jnp.concatenate(
                    [jnp.where(first, mine, theirs), jnp.where(first, theirs, mine)]
                )
                high[e, d], low[e, d] = split(tile)
                t_high[e, d], t_low[e, d] = split(tile.T)


def rotate_left_kernel(place, *refs):
    t_high, t_low = refs[:2]
    panels, outs = refs[2:6], refs[6:]
    parts = [load(p) for p in panels]
    for e in range(4):
        total = None
        for d in range(4):
            term = product((t_high[e, d], t_low[e, d]), parts[d])
            total = term if total is None else total + term
        store(outs[e], total)


def back_left_kernel(place, *refs):
    high, low = refs[:2]
    panels, outs = refs[2:6], refs[6:]
    parts = [load(p) for p in panels]
    for d in range(4):
        total = None
        for e in range(4):
            term = product((high[e, d], low[e, d]), parts[e])
            total = term if total is None else total + term
        store(outs[d], total)


def right_kernel(place, own, away, high, low):
    rows = own.shape[1]
    for s in range(16):
        first = place[C] == 0
        mine, theirs = own[s], away[s]
        tile = jnp.concatenate(
            [jnp.where(first, mine, theirs), jnp.where(first, theirs, mine)]
        )
        at = slice(2 * rows * (s % 2), 2 * rows * (s % 2 + 1))
        high[s // 2, at], low[s // 2, at] = split(tile)


def back_right_kernel(r, place, back, high, low, *outs):
    left = split(back[...])
    zh = lax.rem(place[ZH] + r, 2)
    for f in range(4):
        k = zh * 4 + lax.rem(place[X] + f, 4)
        outs[f][...] = product(left, (high[k], low[k]), (1, 1))


def copies_sent(value, axis):
    n = lax.axis_size(axis)
    copies = jnp.broadcast_to(value[None], (n, *value.shape))
    return lax.all_to_all(copies, axis, 0, 0, tiled=True)


def ring(value, axis, tie=None):
    n = value.shape[0] // 2
    up, down = shift(value, axis, 1), shift(value, axis, -1)
    if tie is not None:
        up, down, tie = lax.optimization_barrier((up, down, tie))
    far = [shift(up[:n], axis, 1), shift(down[n:], axis, -1)]
    return [value, up, down] + far


def gathered(value, axis, by=1):
    return [value] + [shift(value, axis, by * d) for d in (1, 2, 3)]


def body(gradient, first_moment, second_moment, left_basis, right_basis):
    zl, y, c = (lax.axis_index(a) for a in WIDE)
    zh, x = (lax.axis_index(a) for a in NARROW)
    place = jnp.stack([zl, y, c, zh, x]).astype(jnp.int32)
    rows, cols = gradient.shape
    half = cols // 2
    size = 2 * rows

    def swapped(value):
        one, two = value[..., :half], value[..., half:]
        first = c == 0
        other = shift(jnp.where(first, two, one), "c", 1)
        return jnp.concatenate(
            [jnp.where(first, one, other), jnp.where(first, other, two)], -1
        )

    right_z = jnp.stack(
        [right_basis] + [shift(right_basis, "zl", d) for d in (1, 2, 3)]
    )
    (grad,) = call(
        pack_gradient_kernel,
        place,
        [gradient, shift(gradient, "c", 1)],
        [shape(rows, cols)],
    )
    grad = jnp.stack([grad, shift(grad, "zh", 1)])
    grad, right_z = lax.optimization_barrier((grad, right_z))
    left_parts = copies_sent(left_basis, "x")

    (packs,) = call(pack_left_kernel, place, [left_parts], [shape(4, rows, cols)])
    left = lax.all_to_all(packs, "y", 0, 0, tiled=True)
    left, _ = lax.optimization_barrier((left, grad))

    right_parts = ring(right_z, "y")
    grad_parts = ring(grad, "x")
    left_far = shift(left, "zh", 1)
    mine, other, right = call(
        rotate_right_kernel,
        place,
        grad_parts + right_parts,
        [shape(rows, cols)] * 2 + [shape(16, rows, cols)],
        [pltpu.VMEM((8, size, half), BF16)] * 2,
    )
    other, _ = lax.optimization_barrier((other, left_far))
    other = shift(other, "c", 1)
    left_far, other = lax.optimization_barrier((left_far, other))
    rotated_right = mine + other
    both = shift(jnp.stack([left, left_far]), "c", 1)
    lefts = call(
        left_kernel,
        place,
        [left, left_far, both[0], both[1]],
        [shape(4, 4, size, half, dtype=BF16)] * 2
        + [shape(4, 4, half, size, dtype=BF16)] * 2,
    )

    panels = gathered(rotated_right, "y", -1)
    terms = call(
        rotate_left_kernel, place, list(lefts[2:]) + panels, [shape(rows, cols)] * 4
    )
    rotated = terms[0] + sum(shift(terms[e], "zl", e) for e in (1, 2, 3))

    rights = call(
        right_kernel,
        place,
        [right, shift(right, "c", 1)],
        [shape(8, cols, cols, dtype=BF16)] * 2,
    )

    first, second = swapped(jnp.stack([first_moment, second_moment]))
    new_first = beta_first * first + (1.0 - beta_first) * rotated
    new_second = beta_second * second + (1.0 - beta_second) * rotated * rotated
    direction = (
        new_first
        / (1.0 - beta_first**STEP)
        / (jnp.sqrt(new_second / (1.0 - beta_second**STEP)) + epsilon)
    )
    moments = swapped(jnp.stack([new_first, new_second]))

    directions = gathered(direction, "zl", -1)
    lefts, rights = lax.optimization_barrier((lefts, rights))
    back = call(
        back_left_kernel, place, list(lefts[:2]) + directions, [shape(rows, cols)] * 4
    )
    back = swapped(back[0] + sum(shift(back[d], "y", d) for d in (1, 2, 3)))

    def summed(r):
        values = call(
            functools.partial(back_right_kernel, r),
            place,
            [back, *rights],
            [shape(rows, cols)] * 4,
        )
        return values[0] + sum(shift(values[f], "x", f) for f in (1, 2, 3))

    away = shift(summed(1), "zh", 1)
    update = summed(0) + away
    return (update, *moments)


def solution(mesh):
    torus = Mesh(mesh.devices.reshape(4, 4, 2, 2, 4), WIDE + NARROW)
    spec = P(WIDE, NARROW)
    return jax.shard_map(
        body,
        mesh=torus,
        in_specs=(spec,) * 5,
        out_specs=(spec,) * 3,
        check_vma=False,
    )
```

```python
import functools

import jax
import jax.numpy as jnp
from jax import lax
from jax.experimental import pallas as pl
from jax.experimental.pallas import tpu as pltpu
from jax.sharding import Mesh
from jax.sharding import PartitionSpec as P

STEP = 10
WIDE = ("zl", "y", "c")
NARROW = ("zh", "x")

beta_first = 0.9
beta_second = 0.95
epsilon = 1e-08

F32 = jnp.float32
BF16 = jnp.bfloat16


def shift(value, axis, by):
    n = lax.axis_size(axis)
    return lax.ppermute(value, axis, [(i, (i + by) % n) for i in range(n)])


def split(value):
    high = value.astype(BF16)
    return high, (value - high.astype(F32)).astype(BF16)


def product(left, right, dims=(1, 0)):
    def one(a, b):
        return lax.dot_general(
            a, b, (((dims[0],), (dims[1],)), ((), ())), preferred_element_type=F32
        )

    return one(left[0], right[0]) + (one(left[0], right[1]) + one(left[1], right[0]))


def call(kernel, place, arrays, outs, scratch=()):
    return pl.pallas_call(
        kernel,
        out_shape=outs,
        in_specs=[pl.BlockSpec(memory_space=pltpu.SMEM)]
        + [pl.BlockSpec(memory_space=pltpu.VMEM)] * len(arrays),
        out_specs=[pl.BlockSpec(memory_space=pltpu.VMEM)] * len(outs),
        scratch_shapes=scratch,
        compiler_params=pltpu.CompilerParams(vmem_limit_bytes=20 * 2**20),
    )(place, *arrays)


def shape(*lengths, dtype=F32):
    return jax.ShapeDtypeStruct(lengths, dtype)


ZL, Y, C, ZH, X = range(5)


def packed(value):
    rows, half = value.shape[0] // 2, value.shape[1]
    return (slice(0, half), value[:rows]), (slice(half, 2 * half), value[rows:])


def store(ref, value):
    for lanes, part in packed(value):
        ref[:, lanes] = part


def load(ref):
    half = ref.shape[1] // 2
    return split(jnp.concatenate([ref[:, :half], ref[:, half:]]))


def core_columns(tile, which):
    q = tile.shape[1] // 4
    even = jnp.concatenate([tile[:, :q], tile[:, 2 * q : 3 * q]], 1)
    odd = jnp.concatenate([tile[:, q : 2 * q], tile[:, 3 * q :]], 1)
    return jnp.where(which == 0, even, odd)


def pack_gradient_kernel(place, own, away, out):
    half = out.shape[1] // 2
    first = place[C] == 0
    mine = core_columns(own[...], place[C])
    theirs = core_columns(away[...], place[C])
    out[:, :half] = jnp.where(first, mine, theirs)
    out[:, half:] = jnp.where(first, theirs, mine)


def rotate_right_kernel(place, *refs):
    grads, rights = refs[:5], refs[5:10]
    mine, other, right, g_high, g_low = refs[10:]
    rows, cols = right.shape[1], right.shape[2]
    half = cols // 2
    first = place[C] == 0
    for dy in range(4):
        for dz in range(4):
            at = lax.rem(place[ZL] + 4 - dz, 4) * 4 + lax.rem(place[Y] + dy, 4)
            if dy == 2:
                right[at] = rights[3 + dz // 2][dz % 2]
            else:
                right[at] = rights[(0, 2, None, 1)[dy]][dz]
    for dx in range(4):
        x = lax.rem(place[X] + dx, 4)
        for r in range(2):
            at = lax.rem(place[ZH] + r, 2) * 4 + x
            if dx == 2:
                block = grads[3 + r][0]
            else:
                block = grads[(0, 2, None, 1)[dx]][r]
            tile = jnp.concatenate([block[:, :half], block[:, half:]])
            g_high[at], g_low[at] = split(tile)
    total = None
    for k in range(8):
        block = right[2 * k : 2 * k + 2].reshape(2 * rows, cols)
        term = product((g_high[k], g_low[k]), split(block))
        total = term if total is None else total + term
    store(mine, jnp.where(first, total[:, :half], total[:, half:]))
    store(other, jnp.where(first, total[:, half:], total[:, :half]))


def pack_left_kernel(place, stack, out):
    half = out.shape[-1] // 2
    for d in range(4):
        for t in range(2):
            tile = stack[2 * t + d // 2]
            lanes = slice(half * t, half * (t + 1))
            out[d, :, lanes] = tile[:, :half] if d % 2 == 0 else tile[:, half:]


def left_kernel(place, *refs):
    owns, aways = refs[:2], refs[2]
    high, low, t_high, t_low = refs[3:]
    rows, half = owns[0].shape[1], owns[0].shape[2] // 2
    first = place[C] == 0
    for r in range(2):
        for t in range(2):
            a = 2 * lax.rem(place[ZH] + r, 2) + t
            e = lax.rem(a + 4 - place[ZL], 4)
            for d in range(4):
                at = lax.rem(place[Y] + d, 4)
                lanes = slice(half * t, half * (t + 1))
                mine, theirs = owns[r][at, :, lanes], aways[r, at, :, lanes]
                tile = jnp.concatenate(
                    [jnp.where(first, mine, theirs), jnp.where(first, theirs, mine)]
                )
                high[e, d], low[e, d] = split(tile)
                t_high[e, d], t_low[e, d] = split(tile.T)


def rotate_left_kernel(place, *refs):
    t_high, t_low = refs[:2]
    panels, outs = refs[2:6], refs[6:]
    parts = [load(p) for p in panels]
    for e in range(4):
        total = None
        for d in range(4):
            term = product((t_high[e, d], t_low[e, d]), parts[d])
            total = term if total is None else total + term
        store(outs[e], total)


def back_left_kernel(place, *refs):
    high, low = refs[:2]
    panels, outs = refs[2:6], refs[6:]
    parts = [load(p) for p in panels]
    for d in range(4):
        total = None
        for e in range(4):
            term = product((high[e, d], low[e, d]), parts[e])
            total = term if total is None else total + term
        store(outs[d], total)


def right_kernel(place, own, away, high, low):
    rows = own.shape[1]
    for s in range(16):
        first = place[C] == 0
        mine, theirs = own[s], away[s]
        tile = jnp.concatenate(
            [jnp.where(first, mine, theirs), jnp.where(first, theirs, mine)]
        )
        at = slice(2 * rows * (s % 2), 2 * rows * (s % 2 + 1))
        high[s // 2, at], low[s // 2, at] = split(tile)


def back_right_kernel(r, place, back, high, low, *outs):
    left = split(back[...])
    zh = lax.rem(place[ZH] + r, 2)
    for f in range(4):
        k = zh * 4 + lax.rem(place[X] + f, 4)
        outs[f][...] = product(left, (high[k], low[k]), (1, 1))


def copies_sent(value, axis):
    n = lax.axis_size(axis)
    copies = jnp.broadcast_to(value[None], (n, *value.shape))
    return lax.all_to_all(copies, axis, 0, 0, tiled=True)


def ring(value, axis, tie=None):
    n = value.shape[0] // 2
    up, down = shift(value, axis, 1), shift(value, axis, -1)
    if tie is not None:
        up, down, tie = lax.optimization_barrier((up, down, tie))
    far = [shift(up[:n], axis, 1), shift(down[n:], axis, -1)]
    return [value, up, down] + far


def gathered(value, axis, by=1):
    return [value] + [shift(value, axis, by * d) for d in (1, 2, 3)]


def body(gradient, first_moment, second_moment, left_basis, right_basis):
    zl, y, c = (lax.axis_index(a) for a in WIDE)
    zh, x = (lax.axis_index(a) for a in NARROW)
    place = jnp.stack([zl, y, c, zh, x]).astype(jnp.int32)
    rows, cols = gradient.shape
    half = cols // 2
    size = 2 * rows

    def swapped(value):
        one, two = value[..., :half], value[..., half:]
        first = c == 0
        other = shift(jnp.where(first, two, one), "c", 1)
        return jnp.concatenate(
            [jnp.where(first, one, other), jnp.where(first, other, two)], -1
        )

    right_z = jnp.stack(
        [right_basis] + [shift(right_basis, "zl", d) for d in (1, 2, 3)]
    )
    (grad,) = call(
        pack_gradient_kernel,
        place,
        [gradient, shift(gradient, "c", 1)],
        [shape(rows, cols)],
    )
    grad = jnp.stack([grad, shift(grad, "zh", 1)])
    grad, right_z = lax.optimization_barrier((grad, right_z))
    left_parts = copies_sent(left_basis, "x")

    (packs,) = call(pack_left_kernel, place, [left_parts], [shape(4, rows, cols)])
    left = lax.all_to_all(packs, "y", 0, 0, tiled=True)
    left, _ = lax.optimization_barrier((left, grad))

    right_parts = ring(right_z, "y")
    grad_parts = ring(grad, "x")
    left_far = shift(left, "zh", 1)
    mine, other, right = call(
        rotate_right_kernel,
        place,
        grad_parts + right_parts,
        [shape(rows, cols)] * 2 + [shape(16, rows, cols)],
        [pltpu.VMEM((8, size, half), BF16)] * 2,
    )
    other, _ = lax.optimization_barrier((other, left_far))
    other = shift(other, "c", 1)
    rotated_right = mine + other
    left_far, first_moment, second_moment, right, rotated_right = lax.optimization_barrier(
        (left_far, first_moment, second_moment, right, rotated_right)
    )
    both = shift(jnp.stack([left, left_far]), "c", 1)
    lefts = call(
        left_kernel,
        place,
        [left, left_far, both],
        [shape(4, 4, size, half, dtype=BF16)] * 2
        + [shape(4, 4, half, size, dtype=BF16)] * 2,
    )

    panels = gathered(rotated_right, "y", -1)
    terms = call(
        rotate_left_kernel, place, list(lefts[2:]) + panels, [shape(rows, cols)] * 4
    )
    rotated = terms[0] + sum(shift(terms[e], "zl", e) for e in (1, 2, 3))

    rights = call(
        right_kernel,
        place,
        [right, shift(right, "c", 1)],
        [shape(8, cols, cols, dtype=BF16)] * 2,
    )

    first, second = swapped(jnp.stack([first_moment, second_moment]))
    new_first = beta_first * first + (1.0 - beta_first) * rotated
    new_second = beta_second * second + (1.0 - beta_second) * rotated * rotated
    direction = (
        new_first
        / (1.0 - beta_first**STEP)
        / (jnp.sqrt(new_second / (1.0 - beta_second**STEP)) + epsilon)
    )
    moments = swapped(jnp.stack([new_first, new_second]))

    directions = gathered(direction, "zl", -1)
    lefts, rights = lax.optimization_barrier((lefts, rights))
    back = call(
        back_left_kernel, place, list(lefts[:2]) + directions, [shape(rows, cols)] * 4
    )
    back = swapped(back[0] + sum(shift(back[d], "y", d) for d in (1, 2, 3)))

    def summed(r):
        values = call(
            functools.partial(back_right_kernel, r),
            place,
            [back, *rights],
            [shape(rows, cols)] * 4,
        )
        return values[0] + sum(shift(values[f], "x", f) for f in (1, 2, 3))

    away = shift(summed(1), "zh", 1)
    update = summed(0) + away
    return (update, *moments)


def solution(mesh):
    torus = Mesh(mesh.devices.reshape(4, 4, 2, 2, 4), WIDE + NARROW)
    spec = P(WIDE, NARROW)
    return jax.shard_map(
        body,
        mesh=torus,
        in_specs=(spec,) * 5,
        out_specs=(spec,) * 3,
        check_vma=False,
    )
```

```python
import functools

import jax
import jax.numpy as jnp
from jax import lax
from jax.experimental import pallas as pl
from jax.experimental.pallas import tpu as pltpu
from jax.sharding import Mesh
from jax.sharding import PartitionSpec as P

STEP = 10
WIDE = ("zl", "y", "c")
NARROW = ("zh", "x")

beta_first = 0.9
beta_second = 0.95
epsilon = 1e-08

F32 = jnp.float32
BF16 = jnp.bfloat16


def shift(value, axis, by):
    n = lax.axis_size(axis)
    return lax.ppermute(value, axis, [(i, (i + by) % n) for i in range(n)])


def split(value):
    high = value.astype(BF16)
    return high, (value - high.astype(F32)).astype(BF16)


def product(left, right, dims=(1, 0)):
    def one(a, b):
        return lax.dot_general(
            a, b, (((dims[0],), (dims[1],)), ((), ())), preferred_element_type=F32
        )

    return one(left[0], right[0]) + (one(left[0], right[1]) + one(left[1], right[0]))


def call(kernel, place, arrays, outs, scratch=()):
    return pl.pallas_call(
        kernel,
        out_shape=outs,
        in_specs=[pl.BlockSpec(memory_space=pltpu.SMEM)]
        + [pl.BlockSpec(memory_space=pltpu.VMEM)] * len(arrays),
        out_specs=[pl.BlockSpec(memory_space=pltpu.VMEM)] * len(outs),
        scratch_shapes=scratch,
        compiler_params=pltpu.CompilerParams(vmem_limit_bytes=20 * 2**20),
    )(place, *arrays)


def shape(*lengths, dtype=F32):
    return jax.ShapeDtypeStruct(lengths, dtype)


ZL, Y, C, ZH, X = range(5)


def packed(value):
    rows, half = value.shape[0] // 2, value.shape[1]
    return (slice(0, half), value[:rows]), (slice(half, 2 * half), value[rows:])


def store(ref, value):
    for lanes, part in packed(value):
        ref[:, lanes] = part


def load(ref):
    half = ref.shape[1] // 2
    return split(jnp.concatenate([ref[:, :half], ref[:, half:]]))


def core_columns(tile, which):
    q = tile.shape[1] // 4
    even = jnp.concatenate([tile[:, :q], tile[:, 2 * q : 3 * q]], 1)
    odd = jnp.concatenate([tile[:, q : 2 * q], tile[:, 3 * q :]], 1)
    return jnp.where(which == 0, even, odd)


def pack_gradient_kernel(place, own, away, out):
    half = out.shape[1] // 2
    first = place[C] == 0
    mine = core_columns(own[...], place[C])
    theirs = core_columns(away[...], place[C])
    out[:, :half] = jnp.where(first, mine, theirs)
    out[:, half:] = jnp.where(first, theirs, mine)


def rotate_right_kernel(place, *refs):
    grads, rights = refs[:5], refs[5:10]
    mine, other, right, g_high, g_low = refs[10:]
    rows, cols = right.shape[1], right.shape[2]
    half = cols // 2
    first = place[C] == 0
    for dy in range(4):
        for dz in range(4):
            at = lax.rem(place[ZL] + 4 - dz, 4) * 4 + lax.rem(place[Y] + dy, 4)
            if dy == 2:
                right[at] = rights[3 + dz // 2][dz % 2]
            else:
                right[at] = rights[(0, 2, None, 1)[dy]][dz]
    for dx in range(4):
        x = lax.rem(place[X] + dx, 4)
        for r in range(2):
            at = lax.rem(place[ZH] + r, 2) * 4 + x
            if dx == 2:
                block = grads[3 + r][0]
            else:
                block = grads[(0, 2, None, 1)[dx]][r]
            tile = jnp.concatenate([block[:, :half], block[:, half:]])
            g_high[at], g_low[at] = split(tile)
    total = None
    for k in range(8):
        block = right[2 * k : 2 * k + 2].reshape(2 * rows, cols)
        term = product((g_high[k], g_low[k]), split(block))
        total = term if total is None else total + term
    store(mine, jnp.where(first, total[:, :half], total[:, half:]))
    store(other, jnp.where(first, total[:, half:], total[:, :half]))


def pack_left_kernel(place, stack, out):
    half = out.shape[-1] // 2
    for d in range(4):
        for t in range(2):
            tile = stack[2 * t + d // 2]
            lanes = slice(half * t, half * (t + 1))
            out[d, :, lanes] = tile[:, :half] if d % 2 == 0 else tile[:, half:]


def left_kernel(place, *refs):
    owns, aways = refs[:2], refs[2]
    high, low, t_high, t_low = refs[3:]
    rows, half = owns[0].shape[1], owns[0].shape[2] // 2
    first = place[C] == 0
    for r in range(2):
        for t in range(2):
            a = 2 * lax.rem(place[ZH] + r, 2) + t
            e = lax.rem(a + 4 - place[ZL], 4)
            for d in range(4):
                at = lax.rem(place[Y] + d, 4)
                lanes = slice(half * t, half * (t + 1))
                mine, theirs = owns[r][at, :, lanes], aways[r, at, :, lanes]
                tile = jnp.concatenate(
                    [jnp.where(first, mine, theirs), jnp.where(first, theirs, mine)]
                )
                high[e, d], low[e, d] = split(tile)
                t_high[e, d], t_low[e, d] = split(tile.T)


def rotate_left_kernel(place, *refs):
    t_high, t_low = refs[:2]
    panels, outs = refs[2:6], refs[6:]
    parts = [load(p) for p in panels]
    for e in range(4):
        total = None
        for d in range(4):
            term = product((t_high[e, d], t_low[e, d]), parts[d])
            total = term if total is None else total + term
        store(outs[e], total)


def back_left_kernel(place, *refs):
    high, low = refs[:2]
    panels, outs = refs[2:6], refs[6:]
    parts = [load(p) for p in panels]
    for d in range(4):
        total = None
        for e in range(4):
            term = product((high[e, d], low[e, d]), parts[e])
            total = term if total is None else total + term
        store(outs[d], total)


def right_kernel(place, own, away, high, low):
    rows = own.shape[1]
    for s in range(16):
        first = place[C] == 0
        mine, theirs = own[s], away[s]
        tile = jnp.concatenate(
            [jnp.where(first, mine, theirs), jnp.where(first, theirs, mine)]
        )
        at = slice(2 * rows * (s % 2), 2 * rows * (s % 2 + 1))
        high[s // 2, at], low[s // 2, at] = split(tile)


def back_right_kernel(r, place, back, high, low, *outs):
    left = split(back[...])
    zh = lax.rem(place[ZH] + r, 2)
    for f in range(4):
        k = zh * 4 + lax.rem(place[X] + f, 4)
        outs[f][...] = product(left, (high[k], low[k]), (1, 1))


def copies_sent(value, axis):
    n = lax.axis_size(axis)
    copies = jnp.broadcast_to(value[None], (n, *value.shape))
    return lax.all_to_all(copies, axis, 0, 0, tiled=True)


def ring(value, axis, tie=None):
    n = value.shape[0] // 2
    up, down = shift(value, axis, 1), shift(value, axis, -1)
    if tie is not None:
        up, down, tie = lax.optimization_barrier((up, down, tie))
    far = [shift(up[:n], axis, 1), shift(down[n:], axis, -1)]
    return [value, up, down] + far


def gathered(value, axis, by=1):
    return [value] + [shift(value, axis, by * d) for d in (1, 2, 3)]


def body(gradient, first_moment, second_moment, left_basis, right_basis):
    zl, y, c = (lax.axis_index(a) for a in WIDE)
    zh, x = (lax.axis_index(a) for a in NARROW)
    place = jnp.stack([zl, y, c, zh, x]).astype(jnp.int32)
    rows, cols = gradient.shape
    half = cols // 2
    size = 2 * rows

    def swapped(value):
        one, two = value[..., :half], value[..., half:]
        first = c == 0
        other = shift(jnp.where(first, two, one), "c", 1)
        return jnp.concatenate(
            [jnp.where(first, one, other), jnp.where(first, other, two)], -1
        )

    right_z = jnp.stack(
        [right_basis] + [shift(right_basis, "zl", d) for d in (1, 2, 3)]
    )
    (grad,) = call(
        pack_gradient_kernel,
        place,
        [gradient, shift(gradient, "c", 1)],
        [shape(rows, cols)],
    )
    grad = jnp.stack([grad, shift(grad, "zh", 1)])
    grad, right_z = lax.optimization_barrier((grad, right_z))
    left_parts = copies_sent(left_basis, "x")

    (packs,) = call(pack_left_kernel, place, [left_parts], [shape(4, rows, cols)])
    left = lax.all_to_all(packs, "y", 0, 0, tiled=True)
    left, _ = lax.optimization_barrier((left, grad))

    right_parts = ring(right_z, "y")
    grad_parts = ring(grad, "x")
    left_far = shift(left, "zh", 1)
    mine, other, right = call(
        rotate_right_kernel,
        place,
        grad_parts + right_parts,
        [shape(rows, cols)] * 2 + [shape(16, rows, cols)],
        [pltpu.VMEM((8, size, half), BF16)] * 2,
    )
    other, _ = lax.optimization_barrier((other, left_far))
    other = shift(other, "c", 1)
    rotated_right = mine + other
    left_far, first_moment, second_moment, right, rotated_right = lax.optimization_barrier(
        (left_far, first_moment, second_moment, right, rotated_right)
    )
    both = shift(jnp.stack([left, left_far]), "c", 1)
    lefts = call(
        left_kernel,
        place,
        [left, left_far, both],
        [shape(4, 4, size, half, dtype=BF16)] * 2
        + [shape(4, 4, half, size, dtype=BF16)] * 2,
    )

    panels = gathered(rotated_right, "y", -1)
    terms = call(
        rotate_left_kernel, place, list(lefts[2:]) + panels, [shape(rows, cols)] * 4
    )
    rotated = terms[0] + sum(shift(terms[e], "zl", e) for e in (1, 2, 3))

    rights = call(
        right_kernel,
        place,
        [right, shift(right, "c", 1)],
        [shape(8, cols, cols, dtype=BF16)] * 2,
    )

    first, second = swapped(jnp.stack([first_moment, second_moment]))
    new_first = beta_first * first + (1.0 - beta_first) * rotated
    new_second = beta_second * second + (1.0 - beta_second) * rotated * rotated
    direction = (
        new_first
        / (1.0 - beta_first**STEP)
        / (jnp.sqrt(new_second / (1.0 - beta_second**STEP)) + epsilon)
    )
    moments = swapped(jnp.stack([new_first, new_second]))

    directions = gathered(direction, "zl", -1)
    lefts, rights = lax.optimization_barrier((lefts, rights))
    back = call(
        back_left_kernel, place, list(lefts[:2]) + directions, [shape(rows, cols)] * 4
    )
    back = swapped(back[0] + sum(shift(back[d], "y", d) for d in (1, 2, 3)))

    def terms_of(r):
        return call(
            functools.partial(back_right_kernel, r),
            place,
            [back, *rights],
            [shape(rows, cols)] * 4,
        )

    def summed(values):
        return values[0] + sum(shift(values[f], "x", f) for f in (1, 2, 3))

    away, home = summed(terms_of(1)), list(terms_of(0))
    home[3], away = lax.optimization_barrier((home[3], away))
    update = summed(home) + shift(away, "zh", 1)
    return (update, *moments)


def solution(mesh):
    torus = Mesh(mesh.devices.reshape(4, 4, 2, 2, 4), WIDE + NARROW)
    spec = P(WIDE, NARROW)
    return jax.shard_map(
        body,
        mesh=torus,
        in_specs=(spec,) * 5,
        out_specs=(spec,) * 3,
        check_vma=False,
    )
```
